32 devices in a mesh: wide: 8 (over z, y), narrow: 4 (over x, core).
Axes of the slice: x: 2, y: 2, z: 4, core: 2. Of those that a mesh axis runs over, the one named last changes fastest.
Arguments:
- amplitudes: float32 [8, 512, 1024], P('wide', None, 'narrow'), may hold values from -6 to 6
- partner: float32 [64, 2048, 1024], P(None, 'wide', 'narrow'), may hold values from -0.1875 to 0.1875
- gate_block: float32 [8, 8], replicated, may hold values from -2 to 2
- slice_bits: int32 [6], replicated, may hold values from 0 to 1, as said below
- bit_order: int32 [9], replicated, may hold values from 0 to 8, each once
Outputs:
- contracted: float32 [8, 512, 2048], P(None, 'wide', 'narrow')
The draws below stay inside these ranges and needn't reach their ends.
Inputs may be any that keep to these rules, and one draw needn't show every extreme that they name: bit_order is a permutation of 0 to 8. `slice_bits`: each entry is 0 or 1; the bits are never all equal.
All inputs are finite; a program needn't handle non-finite values.
Results may differ from the reference program's by a relative error of at most 0.00007.
Values sent between devices are 32-bit elements; how exact they have to be, the bound alone decides.
A program may use at most 64 MiB of HBM per device.

```python
import jax
import jax.numpy as jnp
from jax import lax

LBITS = 9
ML = 512
MH = 8
Q = 8
K = 1024
N = 2048
SBITS = 6
S = 64


def draw_slice_bits(key, part):
    number = jax.random.randint(key, (), 1, S - 1, dtype=jnp.int32)
    shifts = jnp.arange(SBITS, dtype=jnp.int32)
    return jnp.bitwise_and(jnp.right_shift(number, shifts), 1).astype(jnp.int32)


def level_of(key, dims, split, smallest, high):
    factor_of = 1.0
    for axis_at, shards_of in split:
        steps = jax.random.uniform(jax.random.fold_in(jax.random.fold_in(key, 6), axis_at), (shards_of,), jnp.float32, smallest / len(split), high / len(split))
        factor_of = factor_of * jnp.repeat(jnp.exp(steps), dims[axis_at] // shards_of).reshape((-1,) + (1,) * (len(dims) - 1 - axis_at))
    return factor_of


def centred(own_key, extent, deviation, reach, pieces=(), kind=jnp.bfloat16):
    loudness = level_of(own_key, extent, pieces, -0.22, 0.18) if pieces else 1.0
    array = jax.random.normal(own_key, extent, jnp.float32) * deviation * loudness
    return jnp.minimum(jnp.maximum(array, -reach), reach).astype(kind)


def setup_inputs(seed: int = 0) -> dict:
    arg_keys = jax.random.split(jax.random.key(seed), 6)
    return {
        "amplitudes": centred(arg_keys[0], (MH, ML, K), 1.0, 6.0, ((0, 8), (2, 4)), jnp.float32),
        "partner": centred(arg_keys[1], (S, N, K), K ** -0.5, 0.1875, ((1, 8), (2, 4)), jnp.float32),
        "gate_block": centred(arg_keys[2], (Q, MH), MH ** -0.5, 2.0, (), jnp.float32),
        "slice_bits": draw_slice_bits(jax.random.fold_in(arg_keys[5], 71), 0),
        "bit_order": jax.random.permutation(arg_keys[4], LBITS).astype(jnp.int32),
    }


def source_rows(bit_order, total_rows):
    width = bit_order.shape[0]
    row_ids = jnp.arange(total_rows, dtype=jnp.int32)
    picked = jnp.bitwise_and(jnp.right_shift(row_ids[:, None], bit_order[None, :].astype(jnp.int32)), 1)
    powers = jnp.left_shift(jnp.ones((width,), jnp.int32), jnp.arange(width, dtype=jnp.int32))
    return jnp.sum(picked * powers[None, :], axis=1).astype(jnp.int32)


def slice_number(slice_bits):
    width = slice_bits.shape[0]
    powers = jnp.left_shift(jnp.ones((width,), jnp.int32), jnp.arange(width, dtype=jnp.int32))
    return jnp.sum(slice_bits.astype(jnp.int32) * powers).astype(jnp.int32)


def reference(amplitudes, partner, gate_block, slice_bits, bit_order):
    source = source_rows(bit_order, amplitudes.shape[1])
    reordered = jnp.take(amplitudes, source, axis=1)
    chosen = lax.dynamic_index_in_dim(partner, slice_number(slice_bits), 0, keepdims=False)
    joined = jnp.einsum('hlk,nk->hln', reordered, chosen, precision=lax.Precision.HIGHEST)
    return jnp.einsum('qh,hln->qln', gate_block, joined, precision=lax.Precision.HIGHEST)
```

```python
import functools

import jax
import jax.numpy as jnp
from jax import lax
from jax.experimental import pallas as pl
from jax.experimental.pallas import tpu as pltpu
from jax.sharding import PartitionSpec as P

F32 = jnp.float32
BF16 = jnp.bfloat16


def slice_kernel(bits_ref, partner_ref, chosen_ref):
    chosen_ref[...] = partner_ref[0]


def slice_at(bits_ref):
    number = bits_ref[0]
    for j in range(1, bits_ref.shape[0]):
        number = number + bits_ref[j] * (1 << j)
    return number


def choose(partner, slice_bits):
    _, rows, cols = partner.shape
    return pl.pallas_call(
        slice_kernel,
        out_shape=jax.ShapeDtypeStruct((rows, cols), F32),
        grid_spec=pltpu.PrefetchScalarGridSpec(
            num_scalar_prefetch=1,
            grid=(1,),
            in_specs=[pl.BlockSpec((1, rows, cols), lambda i, bits: (slice_at(bits), 0, 0))],
            out_specs=pl.BlockSpec((rows, cols), lambda i, bits: (0, 0)),
        ),
    )(slice_bits, partner)


def split2(x):
    hi = x.astype(BF16)
    return hi, (x - hi.astype(F32)).astype(BF16)


def dot_nt(a, b):
    return lax.dot_general(a, b, (((1,), (1,)), ((), ())), preferred_element_type=F32)


def kernel(wides, order_ref, gate_ref, amp_ref, chosen_ref, out_ref,
           send_a, recv_a, mixed, mix_hi, mix_lo, held, far_part, near_part,
           core_far, core_near, x_in,
           a_send, a_recv, up_send, down_send, z_recv, y_send, y_recv, rs_send, rs_recv):
    me = lax.axis_index("wide")
    nar = lax.axis_index("narrow")
    lines = wides // 2
    group = wides // 4
    zs_per = lines // 4
    z, y = me // 2, me % 2
    x, c = nar // 2, nar % 2
    core_peer = (me, x * 2 + 1 - c)
    x_peer = (me, (1 - x) * 2 + c)
    y_peer = (z * 2 + 1 - y, nar)
    rows, cols = amp_ref.shape
    out_bits, low_rows, wide_cols = out_ref.shape

    def rc(src, dst, ssem, rsem, dev):
        return pltpu.make_async_remote_copy(
            src_ref=src, dst_ref=dst, send_sem=ssem, recv_sem=rsem,
            device_id=dev, device_id_type=pl.DeviceIdType.MESH)

    barrier = pltpu.get_barrier_semaphore()

    @pl.loop(1, wides)
    def _(s):
        pl.semaphore_signal(barrier, inc=1, device_id=((me + s) % wides, nar),
                            device_id_type=pl.DeviceIdType.MESH)
    for peer in (core_peer, x_peer):
        pl.semaphore_signal(barrier, inc=1, device_id=peer, device_id_type=pl.DeviceIdType.MESH)
    held[me] = chosen_ref[...]
    pl.semaphore_wait(barrier, wides + 1)

    def up(zz):
        slot = held.at[zz * 2 + y]
        return rc(slot, slot, up_send.at[zz], z_recv.at[zz], ((z + 1) % lines * 2 + y, nar))

    def down(zz):
        slot = held.at[zz * 2 + y]
        return rc(slot, slot, down_send.at[zz], z_recv.at[zz], ((z + lines - 1) % lines * 2 + y, nar))

    def across(zz):
        slot = held.at[zz * 2 + y]
        return rc(slot, slot, y_send.at[zz], y_recv.at[zz], y_peer)

    def across_in(zz):
        slot = held.at[zz * 2 + 1 - y]
        return rc(slot, slot, y_send.at[zz], y_recv.at[zz], y_peer)

    @pl.when(z < lines - 1)
    def _():
        up(z).start()

    @pl.when(z > 0)
    def _():
        down(z).start()
    across(z).start()

    row_ids = lax.broadcasted_iota(jnp.int32, (rows, 128), 0)
    source = jnp.zeros((rows, 128), jnp.int32)
    for j in range(order_ref.shape[0]):
        source = source + (lax.shift_right_logical(row_ids, jnp.broadcast_to(order_ref[j], row_ids.shape)) & 1) * (1 << j)
    lane = lax.broadcasted_iota(jnp.int32, (rows, 128), 1)
    onehot = jnp.concatenate(
        [jnp.where(lane + t * 128 == source, 1.0, 0.0).astype(BF16) for t in range(rows // 128)], axis=1)
    amp = amp_ref[...]
    a1 = amp.astype(BF16)
    rest = amp - a1.astype(F32)
    a2 = rest.astype(BF16)
    a3 = (rest - a2.astype(F32)).astype(BF16)
    moved = (jnp.dot(onehot, a3, preferred_element_type=F32)
             + jnp.dot(onehot, a2, preferred_element_type=F32)
             + jnp.dot(onehot, a1, preferred_element_type=F32))
    send_a[...] = moved.reshape(send_a.shape)

    def a_out(to):
        return rc(send_a.at[to], recv_a.at[me], a_send.at[to], a_recv.at[me], (to, nar))

    def a_in(frm):
        return rc(send_a.at[frm], recv_a.at[frm], a_send.at[frm], a_recv.at[frm], (frm, nar))

    @pl.loop(1, wides)
    def _(s):
        a_out((me + s) % wides).start()
    recv_a[me] = send_a[me]

    def line_step(d):
        @pl.when(z - d >= 0)
        def _():
            up(z - d).wait_recv()

            @pl.when(z < lines - 1)
            def _():
                up(z - d).start()
            across(z - d).start()

        @pl.when(z + d < lines)
        def _():
            down(z + d).wait_recv()

            @pl.when(z > 0)
            def _():
                down(z + d).start()
            across(z + d).start()

    line_step(1)

    @pl.loop(1, wides)
    def _(s):
        a_in((me + s) % wides).wait_recv()

    @pl.loop(0, out_bits)
    def _(q):
        acc = gate_ref[q, 0] * recv_a[0]
        for h in range(1, wides):
            acc = acc + gate_ref[q, h] * recv_a[h]
        mixed[q] = acc
    hi, lo = split2(mixed[...].reshape(rows, cols))
    mix_hi[...] = hi
    mix_lo[...] = lo

    def product(o, dst, role):
        @pl.loop(0, zs_per)
        def _(i):
            across_in(o * zs_per + i).wait_recv()
        b = held[pl.ds(o * group, group)].reshape(wide_cols, cols)
        bh, bl = split2(b)
        mh, ml = mix_hi[...], mix_lo[...]
        dst[role] = dot_nt(mh, bl) + dot_nt(ml, bh) + dot_nt(mh, bh)

    def core_send(src, dst, k):
        return rc(src, dst, rs_send.at[k], rs_recv.at[k], core_peer)

    far_core = core_send(far_part.at[1], core_far, 0)
    near_core = core_send(near_part.at[1], core_near, 1)
    over_x = rc(far_part.at[0], x_in, rs_send.at[2], rs_recv.at[2], x_peer)

    def remote_chunk(o):
        role = (o + c) % 2
        product(o, far_part, role)

        @pl.when(role == 1)
        def _():
            far_core.start()

        @pl.when(role == 0)
        def _():
            far_core.wait_recv()
            far_part[0] = far_part[0] + core_far[...]
            over_x.start()

    def local_chunk(o):
        role = (o + c) % 2
        product(o, near_part, role)

        @pl.when(role == 1)
        def _():
            near_core.start()

    here = z // zs_per
    remote_low = (1 - x) * 2
    first = jnp.where(here > remote_low, remote_low + 1, remote_low)
    second = remote_low * 2 + 1 - first
    last_near = 3 * zs_per - 1
    for d in range(2, last_near + 1):
        line_step(d)
    remote_chunk(first)
    for d in range(max(2, last_near + 1), lines):
        line_step(d)
    remote_chunk(second)
    local_chunk(x * 2 + 1 - c)
    local_chunk(nar)
    near_core.wait_recv()
    near_part[0] = near_part[0] + core_near[...]
    over_x.wait_recv()
    out_ref[...] = (near_part[0] + x_in[...]).reshape(out_ref.shape)

    far_core.wait_send()
    near_core.wait_send()
    over_x.wait_send()

    @pl.loop(1, wides)
    def _(s):
        a_out((me + s) % wides).wait_send()
    for zz in range(lines):
        across(zz).wait_send()

        @pl.when((z < lines - 1) & (zz <= z))
        def _():
            up(zz).wait_send()

        @pl.when((z > 0) & (zz >= z))
        def _():
            down(zz).wait_send()


def solution(mesh):
    wides = mesh.shape["wide"]

    def per_device(amplitudes, partner, gate_block, slice_bits, bit_order):
        chosen = choose(partner, slice_bits)
        rows, cols = amplitudes.shape[1:]
        out_bits = gate_block.shape[0]
        low_rows = rows // wides
        block = chosen.shape[0]
        total = block * wides
        own = total // mesh.shape["narrow"]
        flat = out_bits * low_rows
        smem = pl.BlockSpec(memory_space=pltpu.SMEM)
        vmem = pl.BlockSpec(memory_space=pltpu.VMEM)
        dma = pltpu.SemaphoreType.DMA
        lines = wides // 2
        return pl.pallas_call(
            functools.partial(kernel, wides),
            out_shape=jax.ShapeDtypeStruct((out_bits, low_rows, own), F32),
            in_specs=[smem, smem, vmem, vmem],
            out_specs=vmem,
            scratch_shapes=[
                pltpu.VMEM((wides, low_rows, cols), F32),
                pltpu.VMEM((wides, low_rows, cols), F32),
                pltpu.VMEM((out_bits, low_rows, cols), F32),
                pltpu.VMEM((flat, cols), BF16),
                pltpu.VMEM((flat, cols), BF16),
                pltpu.VMEM((wides, block, cols), F32),
                pltpu.VMEM((2, flat, own), F32),
                pltpu.VMEM((2, flat, own), F32),
                pltpu.VMEM((flat, own), F32),
                pltpu.VMEM((flat, own), F32),
                pltpu.VMEM((flat, own), F32),
                dma((wides,)), dma((wides,)),
                dma((lines,)), dma((lines,)), dma((lines,)), dma((lines,)), dma((lines,)),
                dma((3,)), dma((3,)),
            ],
            compiler_params=pltpu.CompilerParams(
                collective_id=0, has_side_effects=True, vmem_limit_bytes=48 * 1024 * 1024),
        )(bit_order, gate_block, amplitudes[0], chosen)

    placed = (P("wide", None, "narrow"), P(None, "wide", "narrow"), P(), P(), P())
    return jax.shard_map(
        per_device, mesh=mesh, in_specs=placed, out_specs=P(None, "wide", "narrow"), check_vma=False
    )
```

```python
import functools

import jax
import jax.numpy as jnp
from jax import lax
from jax.experimental import pallas as pl
from jax.experimental.pallas import tpu as pltpu
from jax.sharding import PartitionSpec as P

F32 = jnp.float32
BF16 = jnp.bfloat16


def slice_kernel(bits_ref, partner_ref, chosen_ref, sem):
    number = bits_ref[0]
    for j in range(1, bits_ref.shape[0]):
        number = number + bits_ref[j] * (1 << j)
    copy = pltpu.make_async_copy(partner_ref.at[number], chosen_ref, sem)
    copy.start()
    copy.wait()


def choose(partner, slice_bits):
    _, rows, cols = partner.shape
    return pl.pallas_call(
        slice_kernel,
        out_shape=jax.ShapeDtypeStruct((rows, cols), F32),
        in_specs=[pl.BlockSpec(memory_space=pltpu.SMEM), pl.BlockSpec(memory_space=pl.ANY)],
        out_specs=pl.BlockSpec(memory_space=pltpu.VMEM),
        scratch_shapes=[pltpu.SemaphoreType.DMA],
    )(slice_bits, partner)


def split2(x):
    hi = x.astype(BF16)
    return hi, (x - hi.astype(F32)).astype(BF16)


def dot_nt(a, b):
    return lax.dot_general(a, b, (((1,), (1,)), ((), ())), preferred_element_type=F32)


PIECES = 4
HALVES = 2


def kernel(wides, order_ref, gate_ref, amp_hbm, chosen_ref, out_ref,
           amp_ref, send_a, recv_a, mixed, mix_hi, mix_lo, held, far_part, near_part,
           core_far, core_near, x_in, amp_sem,
           a_send, a_recv, up_send, down_send, z_recv, y_send, y_recv,
           far_send, far_recv, near_send, near_recv, x_send, x_recv):
    me = lax.axis_index("wide")
    nar = lax.axis_index("narrow")
    lines = wides // 2
    group = wides // 4
    zs_per = lines // 4
    z, y = me // 2, me % 2
    x, c = nar // 2, nar % 2
    core_peer = (me, x * 2 + 1 - c)
    x_peer = (me, (1 - x) * 2 + c)
    y_peer = (z * 2 + 1 - y, nar)
    rows, cols = amp_ref.shape
    out_bits, low_rows, wide_cols = out_ref.shape
    half = held.shape[1] // HALVES
    flat = out_bits * low_rows

    def rc(src, dst, ssem, rsem, dev):
        return pltpu.make_async_remote_copy(
            src_ref=src, dst_ref=dst, send_sem=ssem, recv_sem=rsem,
            device_id=dev, device_id_type=pl.DeviceIdType.MESH)

    barrier = pltpu.get_barrier_semaphore()
    amp_copy = pltpu.make_async_copy(amp_hbm, amp_ref, amp_sem)
    amp_copy.start()

    @pl.loop(1, wides)
    def _(s):
        pl.semaphore_signal(barrier, inc=1, device_id=((me + s) % wides, nar),
                            device_id_type=pl.DeviceIdType.MESH)
    for peer in (core_peer, x_peer):
        pl.semaphore_signal(barrier, inc=1, device_id=peer, device_id_type=pl.DeviceIdType.MESH)
    held[me] = chosen_ref[...]

    row_ids = lax.broadcasted_iota(jnp.int32, (rows, 128), 0)
    source = jnp.zeros((rows, 128), jnp.int32)
    for j in range(order_ref.shape[0]):
        source = source + (lax.shift_right_logical(row_ids, jnp.broadcast_to(order_ref[j], row_ids.shape)) & 1) * (1 << j)
    lane = lax.broadcasted_iota(jnp.int32, (rows, 128), 1)
    onehot = jnp.concatenate(
        [jnp.where(lane + t * 128 == source, 1.0, 0.0).astype(BF16) for t in range(rows // 128)], axis=1)
    amp_copy.wait()
    amp = amp_ref[...]
    a1 = amp.astype(BF16)
    rest = amp - a1.astype(F32)
    a2 = rest.astype(BF16)
    a3 = (rest - a2.astype(F32)).astype(BF16)
    moved = (jnp.dot(onehot, a3, preferred_element_type=F32)
             + jnp.dot(onehot, a2, preferred_element_type=F32)
             + jnp.dot(onehot, a1, preferred_element_type=F32))
    send_a[...] = moved.reshape(send_a.shape)
    pl.semaphore_wait(barrier, wides + 1)

    def slot(w, p):
        return held.at[w, pl.ds(p * half, half)]

    def up(zz, p):
        block = slot(zz * 2 + y, p)
        return rc(block, block, up_send.at[zz, p], z_recv.at[zz, p], ((z + 1) % lines * 2 + y, nar))

    def down(zz, p):
        block = slot(zz * 2 + y, p)
        return rc(block, block, down_send.at[zz, p], z_recv.at[zz, p], ((z + lines - 1) % lines * 2 + y, nar))

    def across(zz, p):
        block = slot(zz * 2 + y, p)
        return rc(block, block, y_send.at[zz, p], y_recv.at[zz, p], y_peer)

    def across_in(zz, p):
        block = slot(zz * 2 + 1 - y, p)
        return rc(block, block, y_send.at[zz, p], y_recv.at[zz, p], y_peer)

    for p in range(HALVES):
        @pl.when(z < lines - 1)
        def _():
            up(z, p).start()

        @pl.when(z > 0)
        def _():
            down(z, p).start()
        across(z, p).start()

    def a_out(to):
        return rc(send_a.at[to], recv_a.at[me], a_send.at[to], a_recv.at[me], (to, nar))

    def a_in(frm):
        return rc(send_a.at[frm], recv_a.at[frm], a_send.at[frm], a_recv.at[frm], (frm, nar))

    @pl.loop(1, wides)
    def _(s):
        a_out((me + s) % wides).start()
    recv_a[me] = send_a[me]

    def line_step(d):
        for p in range(HALVES):
            @pl.when(z - d >= 0)
            def _():
                up(z - d, p).wait_recv()

                @pl.when(z < lines - 1)
                def _():
                    up(z - d, p).start()
                across(z - d, p).start()

            @pl.when(z + d < lines)
            def _():
                down(z + d, p).wait_recv()

                @pl.when(z > 0)
                def _():
                    down(z + d, p).start()
                across(z + d, p).start()

    def product(o, dst, role):
        @pl.loop(0, zs_per)
        def _(i):
            for p in range(HALVES):
                across_in(o * zs_per + i, p).wait_recv()
        b = held[pl.ds(o * group, group)].reshape(wide_cols, cols)
        bh, bl = split2(b)
        mh, ml = mix_hi[...], mix_lo[...]
        dst[role] = dot_nt(mh, bl) + dot_nt(ml, bh) + dot_nt(mh, bh)

    piece = flat // PIECES

    def part(p):
        return pl.ds(p * piece, piece)

    def far_core(p):
        return rc(far_part.at[1, part(p)], core_far.at[part(p)], far_send.at[p], far_recv.at[p], core_peer)

    def over_x(p):
        return rc(far_part.at[0, part(p)], x_in.at[part(p)], x_send.at[p], x_recv.at[p], x_peer)

    near_core = rc(near_part.at[1], core_near, near_send, near_recv, core_peer)

    def remote_chunk(o):
        role = (o + c) % 2
        product(o, far_part, role)

        @pl.when(role == 1)
        def _():
            for p in range(PIECES):
                far_core(p).start()

        @pl.when(role == 0)
        def _():
            for p in range(PIECES):
                far_core(p).wait_recv()
                far_part[0, part(p)] = far_part[0, part(p)] + core_far[part(p)]
                over_x(p).start()

    here = z // zs_per
    remote_low = (1 - x) * 2
    first = jnp.where(here > remote_low, remote_low + 1, remote_low)
    second = remote_low * 2 + 1 - first
    last_near = max(3 * zs_per - 1, 1)
    for d in range(1, last_near + 1):
        line_step(d)

    @pl.loop(1, wides)
    def _(s):
        a_in((me + s) % wides).wait_recv()

    @pl.loop(0, out_bits)
    def _(q):
        acc = gate_ref[q, 0] * recv_a[0]
        for h in range(1, wides):
            acc = acc + gate_ref[q, h] * recv_a[h]
        mixed[q] = acc
    hi, lo = split2(mixed[...].reshape(flat, cols))
    mix_hi[...] = hi
    mix_lo[...] = lo

    remote_chunk(first)
    for d in range(last_near + 1, lines):
        line_step(d)
    remote_chunk(second)
    product(x * 2 + 1 - c, near_part, 1)
    near_core.start()
    product(nar, near_part, 0)
    near_core.wait_recv()
    near_part[0] = near_part[0] + core_near[...]
    for p in range(PIECES):
        over_x(p).wait_recv()
        qs = out_bits // PIECES
        out_ref[p * qs:(p + 1) * qs] = (near_part[0, part(p)] + x_in[part(p)]).reshape(qs, low_rows, wide_cols)

    near_core.wait_send()
    for p in range(PIECES):
        far_core(p).wait_send()
        over_x(p).wait_send()

    @pl.loop(1, wides)
    def _(s):
        a_out((me + s) % wides).wait_send()
    for p in range(HALVES):
        @pl.loop(0, lines)
        def _(zz):
            across(zz, p).wait_send()

            @pl.when((z < lines - 1) & (zz <= z))
            def _():
                up(zz, p).wait_send()

            @pl.when((z > 0) & (zz >= z))
            def _():
                down(zz, p).wait_send()


def solution(mesh):
    wides = mesh.shape["wide"]

    def per_device(amplitudes, partner, gate_block, slice_bits, bit_order):
        chosen = choose(partner, slice_bits)
        rows, cols = amplitudes.shape[1:]
        out_bits = gate_block.shape[0]
        low_rows = rows // wides
        block = chosen.shape[0]
        total = block * wides
        own = total // mesh.shape["narrow"]
        flat = out_bits * low_rows
        smem = pl.BlockSpec(memory_space=pltpu.SMEM)
        vmem = pl.BlockSpec(memory_space=pltpu.VMEM)
        dma = pltpu.SemaphoreType.DMA
        lines = wides // 2
        return pl.pallas_call(
            functools.partial(kernel, wides),
            out_shape=jax.ShapeDtypeStruct((out_bits, low_rows, own), F32),
            in_specs=[smem, smem, pl.BlockSpec(memory_space=pl.ANY), vmem],
            out_specs=vmem,
            scratch_shapes=[
                pltpu.VMEM((rows, cols), F32),
                pltpu.VMEM((wides, low_rows, cols), F32),
                pltpu.VMEM((wides, low_rows, cols), F32),
                pltpu.VMEM((out_bits, low_rows, cols), F32),
                pltpu.VMEM((flat, cols), BF16),
                pltpu.VMEM((flat, cols), BF16),
                pltpu.VMEM((wides, block, cols), F32),
                pltpu.VMEM((2, flat, own), F32),
                pltpu.VMEM((2, flat, own), F32),
                pltpu.VMEM((flat, own), F32),
                pltpu.VMEM((flat, own), F32),
                pltpu.VMEM((flat, own), F32),
                dma,
                dma((wides,)), dma((wides,)),
                *[dma((lines, HALVES))] * 5,
                dma((PIECES,)), dma((PIECES,)), dma, dma, dma((PIECES,)), dma((PIECES,)),
            ],
            compiler_params=pltpu.CompilerParams(
                collective_id=0, has_side_effects=True, vmem_limit_bytes=48 * 1024 * 1024),
        )(bit_order, gate_block, amplitudes[0], chosen)

    placed = (P("wide", None, "narrow"), P(None, "wide", "narrow"), P(), P(), P())
    return jax.shard_map(
        per_device, mesh=mesh, in_specs=placed, out_specs=P(None, "wide", "narrow"), check_vma=False
    )
```

```python
import functools

import jax
import jax.numpy as jnp
from jax import lax
from jax.experimental import pallas as pl
from jax.experimental.pallas import tpu as pltpu
from jax.sharding import PartitionSpec as P

F32 = jnp.float32
BF16 = jnp.bfloat16


def slice_kernel(bits_ref, partner_ref, chosen_ref, sem):
    number = bits_ref[0]
    for j in range(1, bits_ref.shape[0]):
        number = number + bits_ref[j] * (1 << j)
    copy = pltpu.make_async_copy(partner_ref.at[number], chosen_ref, sem)
    copy.start()
    copy.wait()


def choose(partner, slice_bits):
    _, rows, cols = partner.shape
    return pl.pallas_call(
        slice_kernel,
        out_shape=jax.ShapeDtypeStruct((rows, cols), F32),
        in_specs=[pl.BlockSpec(memory_space=pltpu.SMEM), pl.BlockSpec(memory_space=pl.ANY)],
        out_specs=pl.BlockSpec(memory_space=pl.ANY),
        scratch_shapes=[pltpu.SemaphoreType.DMA],
    )(slice_bits, partner)


def split2(x):
    hi = x.astype(BF16)
    return hi, (x - hi.astype(F32)).astype(BF16)


def dot_nt(a, b):
    return lax.dot_general(a, b, (((1,), (1,)), ((), ())), preferred_element_type=F32)


PIECES = 2
HALVES = 2


def kernel(wides, order_ref, gate_ref, amp_hbm, chosen_ref, out_ref,
           amp_ref, send_a, recv_a, mixed, mix_hi, mix_lo, held, far_part, near_part,
           core_far, core_near, x_in, amp_sem, own_sem,
           a_send, a_recv, up_send, down_send, z_recv, y_send, y_recv,
           far_send, far_recv, near_send, near_recv, x_send, x_recv):
    me = lax.axis_index("wide")
    nar = lax.axis_index("narrow")
    lines = wides // 2
    group = wides // 4
    zs_per = lines // 4
    z, y = me // 2, me % 2
    x, c = nar // 2, nar % 2
    core_peer = (me, x * 2 + 1 - c)
    x_peer = (me, (1 - x) * 2 + c)
    y_peer = (z * 2 + 1 - y, nar)
    rows, cols = amp_ref.shape
    out_bits, low_rows, wide_cols = out_ref.shape
    half = held.shape[1] // HALVES
    flat = out_bits * low_rows

    def rc(src, dst, ssem, rsem, dev):
        return pltpu.make_async_remote_copy(
            src_ref=src, dst_ref=dst, send_sem=ssem, recv_sem=rsem,
            device_id=dev, device_id_type=pl.DeviceIdType.MESH)

    barrier = pltpu.get_barrier_semaphore()
    amp_copy = pltpu.make_async_copy(amp_hbm, amp_ref, amp_sem)
    amp_copy.start()
    own_copy = pltpu.make_async_copy(chosen_ref, held.at[me], own_sem)
    own_copy.start()

    @pl.loop(1, wides)
    def _(s):
        pl.semaphore_signal(barrier, inc=1, device_id=((me + s) % wides, nar),
                            device_id_type=pl.DeviceIdType.MESH)
    for peer in (core_peer, x_peer):
        pl.semaphore_signal(barrier, inc=1, device_id=peer, device_id_type=pl.DeviceIdType.MESH)

    row_ids = lax.broadcasted_iota(jnp.int32, (rows, 128), 0)
    source = jnp.zeros((rows, 128), jnp.int32)
    for j in range(order_ref.shape[0]):
        source = source + (lax.shift_right_logical(row_ids, jnp.broadcast_to(order_ref[j], row_ids.shape)) & 1) * (1 << j)
    lane = lax.broadcasted_iota(jnp.int32, (rows, 128), 1)
    onehot = jnp.concatenate(
        [jnp.where(lane + t * 128 == source, 1.0, 0.0).astype(BF16) for t in range(rows // 128)], axis=1)
    amp_copy.wait()
    own_copy.wait()
    amp = amp_ref[...]
    a1 = amp.astype(BF16)
    rest = amp - a1.astype(F32)
    a2 = rest.astype(BF16)
    a3 = (rest - a2.astype(F32)).astype(BF16)
    moved = (jnp.dot(onehot, a3, preferred_element_type=F32)
             + jnp.dot(onehot, a2, preferred_element_type=F32)
             + jnp.dot(onehot, a1, preferred_element_type=F32))
    send_a[...] = moved.reshape(send_a.shape)
    pl.semaphore_wait(barrier, wides + 1)

    def slot(w, p):
        return held.at[w, pl.ds(p * half, half)]

    def up(zz, p):
        block = slot(zz * 2 + y, p)
        return rc(block, block, up_send.at[zz, p], z_recv.at[zz, p], ((z + 1) % lines * 2 + y, nar))

    def down(zz, p):
        block = slot(zz * 2 + y, p)
        return rc(block, block, down_send.at[zz, p], z_recv.at[zz, p], ((z + lines - 1) % lines * 2 + y, nar))

    def across(zz, p):
        block = slot(zz * 2 + y, p)
        return rc(block, block, y_send.at[zz, p], y_recv.at[zz, p], y_peer)

    def across_in(zz, p):
        block = slot(zz * 2 + 1 - y, p)
        return rc(block, block, y_send.at[zz, p], y_recv.at[zz, p], y_peer)

    for p in range(HALVES):
        @pl.when(z < lines - 1)
        def _():
            up(z, p).start()

        @pl.when(z > 0)
        def _():
            down(z, p).start()
        across(z, p).start()

    def a_out(to):
        return rc(send_a.at[to], recv_a.at[me], a_send.at[to], a_recv.at[me], (to, nar))

    def a_in(frm):
        return rc(send_a.at[frm], recv_a.at[frm], a_send.at[frm], a_recv.at[frm], (frm, nar))

    @pl.loop(1, wides)
    def _(s):
        a_out((me + s) % wides).start()
    recv_a[me] = send_a[me]

    def line_step(d):
        for p in range(HALVES):
            @pl.when(z - d >= 0)
            def _():
                up(z - d, p).wait_recv()

                @pl.when(z < lines - 1)
                def _():
                    up(z - d, p).start()
                across(z - d, p).start()

            @pl.when(z + d < lines)
            def _():
                down(z + d, p).wait_recv()

                @pl.when(z > 0)
                def _():
                    down(z + d, p).start()
                across(z + d, p).start()

    subs = far_part.shape[1]

    def cross_wait(o):
        @pl.loop(0, zs_per)
        def _(i):
            for p in range(HALVES):
                across_in(o * zs_per + i, p).wait_recv()

    def times(b):
        bh, bl = split2(b)
        mh, ml = mix_hi[...], mix_lo[...]
        return dot_nt(mh, bl) + dot_nt(ml, bh) + dot_nt(mh, bh)

    def product(o, role):
        cross_wait(o)
        b = held[pl.ds(o * group, group)].reshape(wide_cols, cols)
        near_part[role] = times(b)

    piece = flat // PIECES

    def part(p):
        return pl.ds(p * piece, piece)

    def far_core(v, p):
        return rc(far_part.at[1, v, part(p)], core_far.at[v, part(p)], far_send.at[v, p], far_recv.at[v, p], core_peer)

    def over_x(v, p):
        return rc(far_part.at[0, v, part(p)], x_in.at[v, part(p)], x_send.at[v, p], x_recv.at[v, p], x_peer)

    near_core = rc(near_part.at[1], core_near, near_send, near_recv, core_peer)

    def remote_part(o, turn):
        role = (o + c) % 2
        if subs == 1:
            v = 0
            cross_wait(o)
            b = held[pl.ds(o * group, group)].reshape(wide_cols, cols)
        else:
            v = (y + turn) % 2
            if turn == 1:
                cross_wait(o)
            b = held[o * 2 + v]
        far_part[role, v] = times(b)

        @pl.when(role == 1)
        def _():
            for p in range(PIECES):
                far_core(v, p).start()

        @pl.when(role == 0)
        def _():
            for p in range(PIECES):
                far_core(v, p).wait_recv()
                far_part[0, v, part(p)] = far_part[0, v, part(p)] + core_far[v, part(p)]
                over_x(v, p).start()

    here = z // zs_per
    remote_low = (1 - x) * 2
    first = jnp.where(here > remote_low, remote_low + 1, remote_low)
    second = remote_low * 2 + 1 - first
    last_near = max(3 * zs_per - 1, 1)
    for d in range(1, last_near + 1):
        line_step(d)

    @pl.loop(1, wides)
    def _(s):
        a_in((me + s) % wides).wait_recv()

    @pl.loop(0, out_bits)
    def _(q):
        acc = gate_ref[q, 0] * recv_a[0]
        for h in range(1, wides):
            acc = acc + gate_ref[q, h] * recv_a[h]
        mixed[q] = acc
    hi, lo = split2(mixed[...].reshape(flat, cols))
    mix_hi[...] = hi
    mix_lo[...] = lo

    remote_part(first, 0)
    for d in range(last_near + 1, lines):
        line_step(d)
    for turn in range(1, subs):
        remote_part(first, turn)
    for turn in range(subs):
        remote_part(second, turn)
    product(x * 2 + 1 - c, 1)
    near_core.start()
    product(nar, 0)
    near_core.wait_recv()
    near_part[0] = near_part[0] + core_near[...]
    qs = out_bits // PIECES
    width = wide_cols // subs
    for v in range(subs):
        for p in range(PIECES):
            over_x(v, p).wait_recv()
            out_ref[p * qs:(p + 1) * qs, :, v * width:(v + 1) * width] = (
                near_part[0, part(p), v * width:(v + 1) * width] + x_in[v, part(p)]
            ).reshape(qs, low_rows, width)

    near_core.wait_send()
    for v in range(subs):
        for p in range(PIECES):
            far_core(v, p).wait_send()
            over_x(v, p).wait_send()

    @pl.loop(1, wides)
    def _(s):
        a_out((me + s) % wides).wait_send()
    for p in range(HALVES):
        @pl.loop(0, lines)
        def _(zz):
            across(zz, p).wait_send()

            @pl.when((z < lines - 1) & (zz <= z))
            def _():
                up(zz, p).wait_send()

            @pl.when((z > 0) & (zz >= z))
            def _():
                down(zz, p).wait_send()


def solution(mesh):
    wides = mesh.shape["wide"]

    def per_device(amplitudes, partner, gate_block, slice_bits, bit_order):
        chosen = choose(partner, slice_bits)
        rows, cols = amplitudes.shape[1:]
        out_bits = gate_block.shape[0]
        low_rows = rows // wides
        block = chosen.shape[0]
        total = block * wides
        own = total // mesh.shape["narrow"]
        flat = out_bits * low_rows
        smem = pl.BlockSpec(memory_space=pltpu.SMEM)
        vmem = pl.BlockSpec(memory_space=pltpu.VMEM)
        dma = pltpu.SemaphoreType.DMA
        lines = wides // 2
        subs = 2 if own == 2 * block else 1
        return pl.pallas_call(
            functools.partial(kernel, wides),
            out_shape=jax.ShapeDtypeStruct((out_bits, low_rows, own), F32),
            in_specs=[smem, smem, pl.BlockSpec(memory_space=pl.ANY), pl.BlockSpec(memory_space=pl.ANY)],
            out_specs=vmem,
            scratch_shapes=[
                pltpu.VMEM((rows, cols), F32),
                pltpu.VMEM((wides, low_rows, cols), F32),
                pltpu.VMEM((wides, low_rows, cols), F32),
                pltpu.VMEM((out_bits, low_rows, cols), F32),
                pltpu.VMEM((flat, cols), BF16),
                pltpu.VMEM((flat, cols), BF16),
                pltpu.VMEM((wides, block, cols), F32),
                pltpu.VMEM((2, subs, flat, own // subs), F32),
                pltpu.VMEM((2, flat, own), F32),
                pltpu.VMEM((subs, flat, own // subs), F32),
                pltpu.VMEM((flat, own), F32),
                pltpu.VMEM((subs, flat, own // subs), F32),
                dma, dma,
                dma((wides,)), dma((wides,)),
                *[dma((lines, HALVES))] * 5,
                dma((subs, PIECES)), dma((subs, PIECES)), dma, dma, dma((subs, PIECES)), dma((subs, PIECES)),
            ],
            compiler_params=pltpu.CompilerParams(
                collective_id=0, has_side_effects=True, vmem_limit_bytes=60 * 1024 * 1024),
        )(bit_order, gate_block, amplitudes[0], chosen)

    placed = (P("wide", None, "narrow"), P(None, "wide", "narrow"), P(), P(), P())
    return jax.shard_map(
        per_device, mesh=mesh, in_specs=placed, out_specs=P(None, "wide", "narrow"), check_vma=False
    )
```

```python
import functools

import jax
import jax.numpy as jnp
from jax import lax
from jax.experimental import pallas as pl
from jax.experimental.pallas import tpu as pltpu
from jax.sharding import PartitionSpec as P

F32 = jnp.float32
BF16 = jnp.bfloat16


def slice_kernel(bits_ref, partner_ref, chosen_ref, sem):
    number = bits_ref[0]
    for j in range(1, bits_ref.shape[0]):
        number = number + bits_ref[j] * (1 << j)
    copy = pltpu.make_async_copy(partner_ref.at[number], chosen_ref, sem)
    copy.start()
    copy.wait()


def choose(partner, slice_bits):
    _, rows, cols = partner.shape
    return pl.pallas_call(
        slice_kernel,
        out_shape=pltpu.VMEM((rows, cols), F32),
        in_specs=[pl.BlockSpec(memory_space=pltpu.SMEM), pl.BlockSpec(memory_space=pl.ANY)],
        out_specs=pl.BlockSpec(memory_space=pltpu.VMEM),
        scratch_shapes=[pltpu.SemaphoreType.DMA],
    )(slice_bits, partner)


def split2(x):
    hi = x.astype(BF16)
    return hi, (x - hi.astype(F32)).astype(BF16)


def dot_nt(a, b):
    return lax.dot_general(a, b, (((1,), (1,)), ((), ())), preferred_element_type=F32)


PIECES = 2
HALVES = 2


def kernel(wides, order_ref, gate_ref, amp_hbm, chosen_ref, out_ref,
           amp_ref, send_a, recv_a, mixed, mix_hi, mix_lo, held, far_part, near_part,
           core_far, core_near, x_in, amp_sem, own_sem,
           a_send, a_recv, up_send, down_send, z_recv, y_send, y_recv,
           far_send, far_recv, near_send, near_recv, x_send, x_recv):
    me = lax.axis_index("wide")
    nar = lax.axis_index("narrow")
    lines = wides // 2
    group = wides // 4
    zs_per = lines // 4
    z, y = me // 2, me % 2
    x, c = nar // 2, nar % 2
    core_peer = (me, x * 2 + 1 - c)
    x_peer = (me, (1 - x) * 2 + c)
    y_peer = (z * 2 + 1 - y, nar)
    rows, cols = amp_ref.shape
    out_bits, low_rows, wide_cols = out_ref.shape
    half = held.shape[1] // HALVES
    flat = out_bits * low_rows

    def rc(src, dst, ssem, rsem, dev):
        return pltpu.make_async_remote_copy(
            src_ref=src, dst_ref=dst, send_sem=ssem, recv_sem=rsem,
            device_id=dev, device_id_type=pl.DeviceIdType.MESH)

    barrier = pltpu.get_barrier_semaphore()
    amp_copy = pltpu.make_async_copy(amp_hbm, amp_ref, amp_sem)
    amp_copy.start()
    own_copy = pltpu.make_async_copy(chosen_ref, held.at[me], own_sem)
    own_copy.start()

    @pl.loop(1, wides)
    def _(s):
        pl.semaphore_signal(barrier, inc=1, device_id=((me + s) % wides, nar),
                            device_id_type=pl.DeviceIdType.MESH)
    for peer in (core_peer, x_peer):
        pl.semaphore_signal(barrier, inc=1, device_id=peer, device_id_type=pl.DeviceIdType.MESH)

    row_ids = lax.broadcasted_iota(jnp.int32, (rows, 128), 0)
    source = jnp.zeros((rows, 128), jnp.int32)
    for j in range(order_ref.shape[0]):
        source = source + (lax.shift_right_logical(row_ids, jnp.broadcast_to(order_ref[j], row_ids.shape)) & 1) * (1 << j)
    lane = lax.broadcasted_iota(jnp.int32, (rows, 128), 1)
    onehot = jnp.concatenate(
        [jnp.where(lane + t * 128 == source, 1.0, 0.0).astype(BF16) for t in range(rows // 128)], axis=1)
    amp_copy.wait()
    own_copy.wait()
    amp = amp_ref[...]
    a1 = amp.astype(BF16)
    rest = amp - a1.astype(F32)
    a2 = rest.astype(BF16)
    a3 = (rest - a2.astype(F32)).astype(BF16)
    moved = (jnp.dot(onehot, a3, preferred_element_type=F32)
             + jnp.dot(onehot, a2, preferred_element_type=F32)
             + jnp.dot(onehot, a1, preferred_element_type=F32))
    send_a[...] = moved.reshape(send_a.shape)
    pl.semaphore_wait(barrier, wides + 1)

    def slot(w, p):
        return held.at[w, pl.ds(p * half, half)]

    def up(zz, p):
        block = slot(zz * 2 + y, p)
        return rc(block, block, up_send.at[zz, p], z_recv.at[zz, p], ((z + 1) % lines * 2 + y, nar))

    def down(zz, p):
        block = slot(zz * 2 + y, p)
        return rc(block, block, down_send.at[zz, p], z_recv.at[zz, p], ((z + lines - 1) % lines * 2 + y, nar))

    def across(zz, p):
        block = slot(zz * 2 + y, p)
        return rc(block, block, y_send.at[zz, p], y_recv.at[zz, p], y_peer)

    def across_in(zz, p):
        block = slot(zz * 2 + 1 - y, p)
        return rc(block, block, y_send.at[zz, p], y_recv.at[zz, p], y_peer)

    for p in range(HALVES):
        @pl.when(z < lines - 1)
        def _():
            up(z, p).start()

        @pl.when(z > 0)
        def _():
            down(z, p).start()
        across(z, p).start()

    def a_out(to):
        return rc(send_a.at[to], recv_a.at[me], a_send.at[to], a_recv.at[me], (to, nar))

    def a_in(frm):
        return rc(send_a.at[frm], recv_a.at[frm], a_send.at[frm], a_recv.at[frm], (frm, nar))

    @pl.loop(1, wides)
    def _(s):
        a_out((me + s) % wides).start()
    recv_a[me] = send_a[me]

    def line_step(d):
        for p in range(HALVES):
            @pl.when(z - d >= 0)
            def _():
                up(z - d, p).wait_recv()

                @pl.when(z < lines - 1)
                def _():
                    up(z - d, p).start()
                across(z - d, p).start()

            @pl.when(z + d < lines)
            def _():
                down(z + d, p).wait_recv()

                @pl.when(z > 0)
                def _():
                    down(z + d, p).start()
                across(z + d, p).start()

    subs = far_part.shape[1]

    def cross_wait(o):
        @pl.loop(0, zs_per)
        def _(i):
            for p in range(HALVES):
                across_in(o * zs_per + i, p).wait_recv()

    def times(b):
        bh, bl = split2(b)
        mh, ml = mix_hi[...], mix_lo[...]
        return dot_nt(mh, bl) + dot_nt(ml, bh) + dot_nt(mh, bh)

    def product(o, role):
        cross_wait(o)
        b = held[pl.ds(o * group, group)].reshape(wide_cols, cols)
        near_part[role] = times(b)

    piece = flat // PIECES

    def part(p):
        return pl.ds(p * piece, piece)

    def far_core(v, p):
        return rc(far_part.at[1, v, part(p)], core_far.at[v, part(p)], far_send.at[v, p], far_recv.at[v, p], core_peer)

    def over_x(v, p):
        return rc(far_part.at[0, v, part(p)], x_in.at[v, part(p)], x_send.at[v, p], x_recv.at[v, p], x_peer)

    near_core = rc(near_part.at[1], core_near, near_send, near_recv, core_peer)

    def remote_part(o, turn):
        role = (o + c) % 2
        if subs == 1:
            v = 0
            cross_wait(o)
            b = held[pl.ds(o * group, group)].reshape(wide_cols, cols)
        else:
            v = (y + turn) % 2
            if turn == 1:
                cross_wait(o)
            b = held[o * 2 + v]
        far_part[role, v] = times(b)

        @pl.when(role == 1)
        def _():
            for p in range(PIECES):
                far_core(v, p).start()

        @pl.when(role == 0)
        def _():
            for p in range(PIECES):
                far_core(v, p).wait_recv()
                far_part[0, v, part(p)] = far_part[0, v, part(p)] + core_far[v, part(p)]
                over_x(v, p).start()

    here = z // zs_per
    remote_low = (1 - x) * 2
    first = jnp.where(here > remote_low, remote_low + 1, remote_low)
    second = remote_low * 2 + 1 - first
    last_near = max(3 * zs_per - 1, 1)
    for d in range(1, last_near + 1):
        line_step(d)

    @pl.loop(1, wides)
    def _(s):
        a_in((me + s) % wides).wait_recv()

    @pl.loop(0, out_bits)
    def _(q):
        acc = gate_ref[q, 0] * recv_a[0]
        for h in range(1, wides):
            acc = acc + gate_ref[q, h] * recv_a[h]
        mixed[q] = acc
    hi, lo = split2(mixed[...].reshape(flat, cols))
    mix_hi[...] = hi
    mix_lo[...] = lo

    remote_part(first, 0)
    for d in range(last_near + 1, lines):
        line_step(d)
    for turn in range(1, subs):
        remote_part(first, turn)
    for turn in range(subs):
        remote_part(second, turn)
    product(x * 2 + 1 - c, 1)
    near_core.start()
    product(nar, 0)
    near_core.wait_recv()
    near_part[0] = near_part[0] + core_near[...]
    qs = out_bits // PIECES
    width = wide_cols // subs
    for v in range(subs):
        for p in range(PIECES):
            over_x(v, p).wait_recv()
            out_ref[p * qs:(p + 1) * qs, :, v * width:(v + 1) * width] = (
                near_part[0, part(p), v * width:(v + 1) * width] + x_in[v, part(p)]
            ).reshape(qs, low_rows, width)

    near_core.wait_send()
    for v in range(subs):
        for p in range(PIECES):
            far_core(v, p).wait_send()
            over_x(v, p).wait_send()

    @pl.loop(1, wides)
    def _(s):
        a_out((me + s) % wides).wait_send()
    for p in range(HALVES):
        @pl.loop(0, lines)
        def _(zz):
            across(zz, p).wait_send()

            @pl.when((z < lines - 1) & (zz <= z))
            def _():
                up(zz, p).wait_send()

            @pl.when((z > 0) & (zz >= z))
            def _():
                down(zz, p).wait_send()


def solution(mesh):
    wides = mesh.shape["wide"]

    def per_device(amplitudes, partner, gate_block, slice_bits, bit_order):
        chosen = choose(partner, slice_bits)
        rows, cols = amplitudes.shape[1:]
        out_bits = gate_block.shape[0]
        low_rows = rows // wides
        block = chosen.shape[0]
        total = block * wides
        own = total // mesh.shape["narrow"]
        flat = out_bits * low_rows
        smem = pl.BlockSpec(memory_space=pltpu.SMEM)
        vmem = pl.BlockSpec(memory_space=pltpu.VMEM)
        dma = pltpu.SemaphoreType.DMA
        lines = wides // 2
        subs = 2 if own == 2 * block else 1
        return pl.pallas_call(
            functools.partial(kernel, wides),
            out_shape=jax.ShapeDtypeStruct((out_bits, low_rows, own), F32),
            in_specs=[smem, smem, pl.BlockSpec(memory_space=pl.ANY), pl.BlockSpec(memory_space=pl.ANY)],
            out_specs=vmem,
            scratch_shapes=[
                pltpu.VMEM((rows, cols), F32),
                pltpu.VMEM((wides, low_rows, cols), F32),
                pltpu.VMEM((wides, low_rows, cols), F32),
                pltpu.VMEM((out_bits, low_rows, cols), F32),
                pltpu.VMEM((flat, cols), BF16),
                pltpu.VMEM((flat, cols), BF16),
                pltpu.VMEM((wides, block, cols), F32),
                pltpu.VMEM((2, subs, flat, own // subs), F32),
                pltpu.VMEM((2, flat, own), F32),
                pltpu.VMEM((subs, flat, own // subs), F32),
                pltpu.VMEM((flat, own), F32),
                pltpu.VMEM((subs, flat, own // subs), F32),
                dma, dma,
                dma((wides,)), dma((wides,)),
                *[dma((lines, HALVES))] * 5,
                dma((subs, PIECES)), dma((subs, PIECES)), dma, dma, dma((subs, PIECES)), dma((subs, PIECES)),
            ],
            compiler_params=pltpu.CompilerParams(
                collective_id=0, has_side_effects=True, vmem_limit_bytes=48 * 1024 * 1024),
        )(bit_order, gate_block, amplitudes[0], chosen)

    placed = (P("wide", None, "narrow"), P(None, "wide", "narrow"), P(), P(), P())
    return jax.shard_map(
        per_device, mesh=mesh, in_specs=placed, out_specs=P(None, "wide", "narrow"), check_vma=False
    )
```

```python
import functools

import jax
import jax.numpy as jnp
from jax import lax
from jax.experimental import pallas as pl
from jax.experimental.pallas import tpu as pltpu
from jax.sharding import PartitionSpec as P

F32 = jnp.float32
BF16 = jnp.bfloat16


def slice_kernel(bits_ref, partner_ref, chosen_ref, sem):
    number = bits_ref[0]
    for j in range(1, bits_ref.shape[0]):
        number = number + bits_ref[j] * (1 << j)
    copy = pltpu.make_async_copy(partner_ref.at[number], chosen_ref, sem)
    copy.start()
    copy.wait()


def choose(partner, slice_bits):
    _, rows, cols = partner.shape
    return pl.pallas_call(
        slice_kernel,
        out_shape=pltpu.VMEM((rows, cols), F32),
        in_specs=[pl.BlockSpec(memory_space=pltpu.SMEM), pl.BlockSpec(memory_space=pl.ANY)],
        out_specs=pl.BlockSpec(memory_space=pltpu.VMEM),
        scratch_shapes=[pltpu.SemaphoreType.DMA],
    )(slice_bits, partner)


def split2(x):
    hi = x.astype(BF16)
    return hi, (x - hi.astype(F32)).astype(BF16)


def dot_nt(a, b):
    return lax.dot_general(a, b, (((1,), (1,)), ((), ())), preferred_element_type=F32)


PIECES = 2
HALVES = 2


def kernel(wides, order_ref, gate_ref, amp_hbm, chosen_ref, out_ref,
           amp_ref, send_a, recv_a, mixed, mix_hi, mix_lo, held, far_part, near_part,
           core_far, core_near, x_in, amp_sem, own_sem,
           a_send, a_recv, up_send, down_send, z_recv, y_send, y_recv,
           far_send, far_recv, near_send, near_recv, x_send, x_recv):
    me = lax.axis_index("wide")
    nar = lax.axis_index("narrow")
    lines = wides // 2
    group = wides // 4
    zs_per = lines // 4
    z, y = me // 2, me % 2
    x, c = nar // 2, nar % 2
    core_peer = (me, x * 2 + 1 - c)
    x_peer = (me, (1 - x) * 2 + c)
    y_peer = (z * 2 + 1 - y, nar)
    rows, cols = amp_ref.shape
    out_bits, low_rows, wide_cols = out_ref.shape
    half = held.shape[1] // HALVES
    flat = out_bits * low_rows

    def rc(src, dst, ssem, rsem, dev):
        return pltpu.make_async_remote_copy(
            src_ref=src, dst_ref=dst, send_sem=ssem, recv_sem=rsem,
            device_id=dev, device_id_type=pl.DeviceIdType.MESH)

    barrier = pltpu.get_barrier_semaphore()
    amp_copy = pltpu.make_async_copy(amp_hbm, amp_ref, amp_sem)
    amp_copy.start()
    own_copy = pltpu.make_async_copy(chosen_ref, held.at[me], own_sem)
    own_copy.start()

    @pl.loop(1, wides)
    def _(s):
        pl.semaphore_signal(barrier, inc=1, device_id=((me + s) % wides, nar),
                            device_id_type=pl.DeviceIdType.MESH)
    for peer in (core_peer, x_peer):
        pl.semaphore_signal(barrier, inc=1, device_id=peer, device_id_type=pl.DeviceIdType.MESH)

    row_ids = lax.broadcasted_iota(jnp.int32, (rows, 128), 0)
    source = jnp.zeros((rows, 128), jnp.int32)
    for j in range(order_ref.shape[0]):
        source = source + (lax.shift_right_logical(row_ids, jnp.broadcast_to(order_ref[j], row_ids.shape)) & 1) * (1 << j)
    lane = lax.broadcasted_iota(jnp.int32, (rows, 128), 1)
    onehot = jnp.concatenate(
        [jnp.where(lane + t * 128 == source, 1.0, 0.0).astype(BF16) for t in range(rows // 128)], axis=1)
    amp_copy.wait()
    own_copy.wait()
    amp = amp_ref[...]
    a1 = amp.astype(BF16)
    rest = amp - a1.astype(F32)
    a2 = rest.astype(BF16)
    a3 = (rest - a2.astype(F32)).astype(BF16)
    moved = (jnp.dot(onehot, a3, preferred_element_type=F32)
             + jnp.dot(onehot, a2, preferred_element_type=F32)
             + jnp.dot(onehot, a1, preferred_element_type=F32))
    send_a[...] = moved.reshape(send_a.shape)
    pl.semaphore_wait(barrier, wides + 1)

    def slot(w, p):
        return held.at[w, pl.ds(p * half, half)]

    def up(zz, p):
        block = slot(zz * 2 + y, p)
        return rc(block, block, up_send.at[zz, p], z_recv.at[zz, p], ((z + 1) % lines * 2 + y, nar))

    def down(zz, p):
        block = slot(zz * 2 + y, p)
        return rc(block, block, down_send.at[zz, p], z_recv.at[zz, p], ((z + lines - 1) % lines * 2 + y, nar))

    def across(zz, p):
        block = slot(zz * 2 + y, p)
        return rc(block, block, y_send.at[zz, p], y_recv.at[zz, p], y_peer)

    def across_in(zz, p):
        block = slot(zz * 2 + 1 - y, p)
        return rc(block, block, y_send.at[zz, p], y_recv.at[zz, p], y_peer)

    for p in range(HALVES):
        @pl.when(z < lines - 1)
        def _():
            up(z, p).start()

        @pl.when(z > 0)
        def _():
            down(z, p).start()
        across(z, p).start()

    def a_out(to):
        return rc(send_a.at[to], recv_a.at[me], a_send.at[to], a_recv.at[me], (to, nar))

    def a_in(frm):
        return rc(send_a.at[frm], recv_a.at[frm], a_send.at[frm], a_recv.at[frm], (frm, nar))

    @pl.loop(1, wides)
    def _(s):
        a_out((me + s) % wides).start()
    recv_a[me] = send_a[me]

    def line_step(d):
        for p in range(HALVES):
            @pl.when(z - d >= 0)
            def _():
                up(z - d, p).wait_recv()

                @pl.when(z < lines - 1)
                def _():
                    up(z - d, p).start()
                across(z - d, p).start()

            @pl.when(z + d < lines)
            def _():
                down(z + d, p).wait_recv()

                @pl.when(z > 0)
                def _():
                    down(z + d, p).start()
                across(z + d, p).start()

    subs = far_part.shape[1]

    def cross_wait(o):
        @pl.loop(0, zs_per)
        def _(i):
            for p in range(HALVES):
                across_in(o * zs_per + i, p).wait_recv()

    def times(b):
        bh, bl = split2(b)
        mh, ml = mix_hi[...], mix_lo[...]
        return dot_nt(mh, bl) + dot_nt(ml, bh) + dot_nt(mh, bh)

    def product(o, role):
        cross_wait(o)
        b = held[pl.ds(o * group, group)].reshape(wide_cols, cols)
        near_part[role] = times(b)

    piece = flat // PIECES

    def part(p):
        return pl.ds(p * piece, piece)

    def far_core(v, p):
        return rc(far_part.at[1, v, part(p)], core_far.at[v, part(p)], far_send.at[v, p], far_recv.at[v, p], core_peer)

    def over_x(v, p):
        return rc(far_part.at[0, v, part(p)], x_in.at[v, part(p)], x_send.at[v, p], x_recv.at[v, p], x_peer)

    near_core = rc(near_part.at[1], core_near, near_send, near_recv, core_peer)

    def remote_part(o, turn):
        role = (o + c) % 2
        if subs == 1:
            v = 0
            cross_wait(o)
            b = held[pl.ds(o * group, group)].reshape(wide_cols, cols)
        else:
            v = (y + turn) % 2
            if turn == 1:
                cross_wait(o)
            b = held[o * 2 + v]
        far_part[role, v] = times(b)

        @pl.when(role == 1)
        def _():
            for p in range(PIECES):
                far_core(v, p).start()

        @pl.when(role == 0)
        def _():
            for p in range(PIECES):
                far_core(v, p).wait_recv()
                far_part[0, v, part(p)] = far_part[0, v, part(p)] + core_far[v, part(p)]
                over_x(v, p).start()

    here = z // zs_per
    remote_low = (1 - x) * 2
    first = jnp.where(here > remote_low, remote_low + 1, remote_low)
    second = remote_low * 2 + 1 - first
    last_near = max(3 * zs_per - 1, 1)
    line_step(1)

    @pl.loop(1, wides)
    def _(s):
        a_in((me + s) % wides).wait_recv()

    @pl.loop(0, out_bits)
    def _(q):
        acc = gate_ref[q, 0] * recv_a[0]
        for h in range(1, wides):
            acc = acc + gate_ref[q, h] * recv_a[h]
        mixed[q] = acc
    hi, lo = split2(mixed[...].reshape(flat, cols))
    mix_hi[...] = hi
    mix_lo[...] = lo

    for d in range(2, last_near + 1):
        line_step(d)
    remote_part(first, 0)
    for d in range(last_near + 1, lines):
        line_step(d)
    for turn in range(1, subs):
        remote_part(first, turn)
    for turn in range(subs):
        remote_part(second, turn)
    product(x * 2 + 1 - c, 1)
    near_core.start()
    product(nar, 0)
    near_core.wait_recv()
    near_part[0] = near_part[0] + core_near[...]
    qs = out_bits // PIECES
    width = wide_cols // subs
    for v in range(subs):
        for p in range(PIECES):
            over_x(v, p).wait_recv()
            out_ref[p * qs:(p + 1) * qs, :, v * width:(v + 1) * width] = (
                near_part[0, part(p), v * width:(v + 1) * width] + x_in[v, part(p)]
            ).reshape(qs, low_rows, width)

    near_core.wait_send()
    for v in range(subs):
        for p in range(PIECES):
            far_core(v, p).wait_send()
            over_x(v, p).wait_send()

    @pl.loop(1, wides)
    def _(s):
        a_out((me + s) % wides).wait_send()
    for p in range(HALVES):
        @pl.loop(0, lines)
        def _(zz):
            across(zz, p).wait_send()

            @pl.when((z < lines - 1) & (zz <= z))
            def _():
                up(zz, p).wait_send()

            @pl.when((z > 0) & (zz >= z))
            def _():
                down(zz, p).wait_send()


def solution(mesh):
    wides = mesh.shape["wide"]

    def per_device(amplitudes, partner, gate_block, slice_bits, bit_order):
        chosen = choose(partner, slice_bits)
        rows, cols = amplitudes.shape[1:]
        out_bits = gate_block.shape[0]
        low_rows = rows // wides
        block = chosen.shape[0]
        total = block * wides
        own = total // mesh.shape["narrow"]
        flat = out_bits * low_rows
        smem = pl.BlockSpec(memory_space=pltpu.SMEM)
        vmem = pl.BlockSpec(memory_space=pltpu.VMEM)
        dma = pltpu.SemaphoreType.DMA
        lines = wides // 2
        subs = 2 if own == 2 * block else 1
        return pl.pallas_call(
            functools.partial(kernel, wides),
            out_shape=jax.ShapeDtypeStruct((out_bits, low_rows, own), F32),
            in_specs=[smem, smem, pl.BlockSpec(memory_space=pl.ANY), pl.BlockSpec(memory_space=pl.ANY)],
            out_specs=vmem,
            scratch_shapes=[
                pltpu.VMEM((rows, cols), F32),
                pltpu.VMEM((wides, low_rows, cols), F32),
                pltpu.VMEM((wides, low_rows, cols), F32),
                pltpu.VMEM((out_bits, low_rows, cols), F32),
                pltpu.VMEM((flat, cols), BF16),
                pltpu.VMEM((flat, cols), BF16),
                pltpu.VMEM((wides, block, cols), F32),
                pltpu.VMEM((2, subs, flat, own // subs), F32),
                pltpu.VMEM((2, flat, own), F32),
                pltpu.VMEM((subs, flat, own // subs), F32),
                pltpu.VMEM((flat, own), F32),
                pltpu.VMEM((subs, flat, own // subs), F32),
                dma, dma,
                dma((wides,)), dma((wides,)),
                *[dma((lines, HALVES))] * 5,
                dma((subs, PIECES)), dma((subs, PIECES)), dma, dma, dma((subs, PIECES)), dma((subs, PIECES)),
            ],
            compiler_params=pltpu.CompilerParams(
                collective_id=0, has_side_effects=True, vmem_limit_bytes=48 * 1024 * 1024),
        )(bit_order, gate_block, amplitudes[0], chosen)

    placed = (P("wide", None, "narrow"), P(None, "wide", "narrow"), P(), P(), P())
    return jax.shard_map(
        per_device, mesh=mesh, in_specs=placed, out_specs=P(None, "wide", "narrow"), check_vma=False
    )
```
